32 devices in a mesh: cluster: 2 (over x), sub: 16 (over z, y, core).
Axes of the slice: x: 2, y: 2, z: 4, core: 2. Of those that a mesh axis runs over, the one named last changes fastest.
Arguments:
- load_terms: float32 [32, 128, 1536], P(('cluster', 'sub')), may hold values from -60 to 60
- dual_operator: bfloat16 [32, 1536, 1536], P(('cluster', 'sub')), may hold values from -2 to 16, as said below
- dirichlet: bfloat16 [32, 1536, 1536], P(('cluster', 'sub')), may hold values from -2 to 16, as said below
- corner_coupling: bfloat16 [32, 1536, 24], P(('cluster', 'sub')), may hold values from -0.25 to 0.25
- coarse_inverse: float32 [96, 96], P(('cluster', 'sub')), may hold values from -2 to 4, as said below
- face_map: int32 [32, 6, 256], P(('cluster', 'sub')), may hold values from 0 to 255, as said below
- face_live: int32 [32, 6], P(('cluster', 'sub')), may hold values from 0 to 1, as said below
- corner_ids: int32 [32, 8], P(('cluster', 'sub')), may hold values from 0 to 31, as said below
Outputs:
- multipliers: float32 [32, 128, 1536], P(('cluster', 'sub'))
- residual: float32 [32, 128, 1536], P(('cluster', 'sub'))
The draws below stay inside these ranges and needn't reach their ends.
Inputs may be any that keep to these rules, and one draw needn't show every extreme that they name: face_map[d, f] is a permutation of the slots of a face; the maps of the two sides of a face pair are inverse to each other. `face_live`: equal on the two sides of a face pair. `corner_ids`: the eight corners of a subdomain are the lattice vertices (c + a, s + b + 4 * e) for a, b, e in 0 and 1, taken modulo 2 and 16; each vertex has one number and is shared by eight subdomains. `dual_operator`: each subdomain's matrix is symmetric and positive definite. `dirichlet`: each subdomain's matrix is symmetric and positive definite. `coarse_inverse`: symmetric and positive definite.
All inputs are finite; a program needn't handle non-finite values.
Results may differ from the reference program's by a relative error of at most 0.0099.
Values sent between devices are 32-bit elements; how exact they have to be, the bound alone decides.
No kernel may reach another device: no remote copies, remote signals or barrier semaphores. Data moves between devices by JAX's collectives and lax.ppermute only.
A program may use at most 128 MiB of HBM per device.

```python
import math
import jax
import jax.numpy as jnp
from jax import lax

FACE = 256
ORDER = 1536
LOADS = 128
ITERS = 2
STRIDE = 4
CORNERS = 8
SLABS = 2
CYCLE = 16
SUBDOMAINS = 32
COARSE = 96


def symmetric_block(key, length, diag_low, diag_high, offdiag):
    first_key, second_key = jax.random.split(key, 2)
    normal = jax.random.normal(first_key, (length, length), jnp.float32)
    offpart = (normal + normal.T) * (offdiag / math.sqrt(2.0 * length))
    diagonal = jax.random.uniform(second_key, (length,), jnp.float32, diag_low, diag_high)
    matrix = offpart + jnp.diag(diagonal)
    return matrix


def draw_dual_operator(key, part):

    def single(position):
        return symmetric_block(jax.random.fold_in(key, position), ORDER, 2.0, 4.0, 0.7).astype(jnp.bfloat16)
    return lax.map(single, jnp.arange(SUBDOMAINS, dtype=jnp.int32))


def draw_dirichlet(key, part):
    base_key = jax.random.fold_in(key, 7)

    def single(position):
        return symmetric_block(jax.random.fold_in(base_key, position), ORDER, 1.5, 3.5, 0.6).astype(jnp.bfloat16)
    return lax.map(single, jnp.arange(SUBDOMAINS, dtype=jnp.int32))


def draw_coarse_inverse(key, part):
    return symmetric_block(jax.random.fold_in(key, 3), COARSE, 0.6, 1.6, 0.25)


def draw_load_terms(key, part):
    subkeys = jax.random.split(key, 3)
    values = jnp.clip(jax.random.normal(subkeys[0], (SUBDOMAINS, LOADS, ORDER), jnp.float32), -4.0, 4.0)
    device_scale = 0.6 + 1.2 * jnp.arange(SUBDOMAINS, dtype=jnp.float32) / (SUBDOMAINS - 1)
    column_scale = jnp.exp(jax.random.uniform(subkeys[1], (LOADS,), jnp.float32, math.log(0.3), math.log(3.0)))
    row_scale = jnp.exp(jax.random.uniform(subkeys[2], (ORDER,), jnp.float32, math.log(0.3), math.log(3.0)))
    values = values * device_scale[:, None, None] * column_scale[None, :, None] * row_scale[None, None, :]
    return jnp.clip(values, -60.0, 60.0)


def face_pairs():
    device = jnp.arange(SUBDOMAINS, dtype=jnp.int32)
    column = device // CYCLE
    within = device % CYCLE
    return jnp.stack([(column - 1) % SLABS * CYCLE + within, device, SUBDOMAINS + column * CYCLE + (within - 1) % CYCLE, SUBDOMAINS + device, 2 * SUBDOMAINS + column * CYCLE + (within - STRIDE) % CYCLE, 2 * SUBDOMAINS + device], axis=1)


def draw_face_map(key, part):
    pair_ids = face_pairs()

    def permute(pair_id):
        return jax.random.permutation(jax.random.fold_in(key, pair_id), FACE).astype(jnp.int32)
    permutations = jax.vmap(jax.vmap(permute))(pair_ids)
    inverse = jnp.argsort(permutations, axis=-1, stable=True).astype(jnp.int32)
    odd_faces = (jnp.arange(6, dtype=jnp.int32) % 2 == 1)[None, :, None]
    return jnp.where(odd_faces, permutations, inverse).astype(jnp.int32)


def draw_face_live(key, part):
    pair_ids = face_pairs()
    base_key = jax.random.fold_in(key, 11)

    def face_alive(pair_id):
        return (jax.random.randint(jax.random.fold_in(base_key, pair_id), (), 0, 4) > 0).astype(jnp.int32)
    return jax.vmap(jax.vmap(face_alive))(pair_ids)


def draw_corner_ids(key, part):
    numbering = jax.random.permutation(jax.random.fold_in(key, 5), SUBDOMAINS).astype(jnp.int32)
    device = jnp.arange(SUBDOMAINS, dtype=jnp.int32)
    column = device // CYCLE
    within = device % CYCLE
    corner = jnp.arange(8, dtype=jnp.int32)
    step_first = corner // 4
    step_second = corner // 2 % 2
    step_third = corner % 2
    vertex = (column[:, None] + step_first[None, :]) % SLABS * CYCLE + (within[:, None] + step_second[None, :] + STRIDE * step_third[None, :]) % CYCLE
    return jnp.take(numbering, vertex).astype(jnp.int32)


def steps_of(key, dims, cuts, smallest, largest):
    factor_of, own = 1.0, jax.random.fold_in(key, 6)
    for axis_at, blocks in cuts:
        heights = jnp.exp(jax.random.uniform(jax.random.fold_in(own, axis_at), (blocks,), jnp.float32, smallest / len(cuts), largest / len(cuts)))
        factor_of = factor_of * jnp.repeat(heights, dims[axis_at] // blocks).reshape([-1 if axis == axis_at else 1 for axis in range(len(dims))])
    return factor_of


def gaussian(stream_key, extent, spread, bound, cuts=(), held_as=jnp.bfloat16):
    gain = steps_of(stream_key, extent, cuts, -0.22, 0.18) if cuts else 1.0
    entries = jax.random.normal(stream_key, extent, jnp.float32) * spread * gain
    return jnp.minimum(jnp.maximum(entries, -bound), bound).astype(held_as)


def setup_inputs(seed: int = 0) -> dict:
    key_of = jax.random.split(jax.random.key(seed), 9)
    load_terms = draw_load_terms(jax.random.fold_in(key_of[8], 71), 0)
    dual_operator = draw_dual_operator(jax.random.fold_in(key_of[8], 71), 0)
    dirichlet = draw_dirichlet(jax.random.fold_in(key_of[8], 71), 0)
    corner_coupling = gaussian(key_of[3], (SUBDOMAINS, ORDER, 3 * CORNERS), (ORDER // 3) ** -0.5, 0.25, ((0, 32),))
    coarse_inverse = draw_coarse_inverse(jax.random.fold_in(key_of[8], 71), 0)
    face_map = draw_face_map(jax.random.fold_in(key_of[8], 71), 0)
    face_live = draw_face_live(jax.random.fold_in(key_of[8], 71), 0)
    corner_ids = draw_corner_ids(jax.random.fold_in(key_of[8], 71), 0)
    return dict(load_terms=load_terms, dual_operator=dual_operator, dirichlet=dirichlet, corner_coupling=corner_coupling, coarse_inverse=coarse_inverse, face_map=face_map, face_live=face_live, corner_ids=corner_ids)


def neighbour_table():
    device = jnp.arange(SUBDOMAINS, dtype=jnp.int32)
    column = device // CYCLE
    within = device % CYCLE
    return jnp.stack([((column - 1) % SLABS) * CYCLE + within, ((column + 1) % SLABS) * CYCLE + within, column * CYCLE + (within - 1) % CYCLE, column * CYCLE + (within + 1) % CYCLE, column * CYCLE + (within - STRIDE) % CYCLE, column * CYCLE + (within + STRIDE) % CYCLE], axis=1)


def assemble(field, neighbours, face_map, face_live):
    face_parts = field.reshape(SUBDOMAINS, LOADS, 6, FACE)
    pieces = []
    for face_index in range(6):
        partner = face_index ^ 1
        source = jnp.take(face_parts[:, :, partner, :], neighbours[:, face_index], axis=0)
        permuted = jnp.take_along_axis(source, face_map[:, face_index][:, None, :], axis=2)
        live_weight = face_live[:, face_index].astype(jnp.float32)[:, None, None]
        pieces.append((face_parts[:, :, face_index, :] + permuted) * live_weight)
    return jnp.stack(pieces, axis=2).reshape(SUBDOMAINS, LOADS, ORDER)


def inner_product(first_field, second_field):
    return 0.5 * jnp.sum(first_field * second_field, axis=(0, 2))


def single_product(operand_pair):
    return jnp.dot(operand_pair[0].astype(jnp.float32), operand_pair[1].astype(jnp.float32), precision=lax.Precision.HIGHEST)


def local_product(rounded, matrices):
    return lax.map(single_product, (rounded, matrices))


def reference(load_terms, dual_operator, dirichlet, corner_coupling, coarse_inverse, face_map, face_live, corner_ids):
    neighbours = neighbour_table()
    coarse_index = (3 * corner_ids[:, :, None] + jnp.arange(3, dtype=jnp.int32)[None, None, :]).reshape(SUBDOMAINS, 3 * CORNERS)
    flat_index = coarse_index.reshape(-1)
    coupling_wide = corner_coupling.astype(jnp.float32)

    def apply_dual(vector):
        rounded = lax.optimization_barrier(vector.astype(jnp.bfloat16))
        direct = local_product(rounded, dual_operator)
        corner_terms = jnp.einsum("dkm,dmc->dkc", rounded.astype(jnp.float32), coupling_wide, precision=lax.Precision.HIGHEST)
        coarse_load = jnp.zeros((LOADS, COARSE), jnp.float32).at[:, flat_index].add(jnp.transpose(corner_terms, (1, 0, 2)).reshape(LOADS, SUBDOMAINS * 3 * CORNERS))
        coarse_field = jnp.dot(coarse_load, coarse_inverse.T, precision=lax.Precision.HIGHEST)
        picked = jnp.take(coarse_field, flat_index, axis=1).reshape(LOADS, SUBDOMAINS, 3 * CORNERS)
        picked = jnp.transpose(picked, (1, 0, 2))
        corner_values = lax.optimization_barrier(picked.astype(jnp.bfloat16))
        back = jnp.einsum("dkc,dmc->dkm", corner_values.astype(jnp.float32), coupling_wide, precision=lax.Precision.HIGHEST)
        return assemble(direct + back, neighbours, face_map, face_live)

    def apply_precond(vector):
        rounded = lax.optimization_barrier(vector.astype(jnp.bfloat16))
        return assemble(local_product(rounded, dirichlet), neighbours, face_map, face_live)

    right_side = assemble(load_terms, neighbours, face_map, face_live)
    multipliers = jnp.zeros_like(right_side)
    residual = right_side
    precond = apply_precond(residual)
    residual_dot = inner_product(residual, precond)
    direction = precond
    for iteration in range(ITERS):
        dual_image = apply_dual(direction)
        step_size = residual_dot / inner_product(direction, dual_image)
        multipliers = multipliers + step_size[None, :, None] * direction
        residual = residual - step_size[None, :, None] * dual_image
        if iteration + 1 < ITERS:
            precond = apply_precond(residual)
            residual_new = inner_product(residual, precond)
            direction = precond + (residual_new / residual_dot)[None, :, None] * direction
            residual_dot = residual_new
    return multipliers, residual
```

```python
import functools

import jax
import jax.numpy as jnp
from jax import lax
from jax.experimental import pallas as pl
from jax.experimental.pallas import tpu as pltpu
from jax.sharding import PartitionSpec as P

ITERS = 2
STRIDE = 4
LANES = 128
AXES = ("cluster", "sub")
EXACT = lax.Precision.HIGHEST
F32 = jnp.float32
BF16 = jnp.bfloat16
VMEM = pl.BlockSpec(memory_space=pltpu.VMEM)
SMEM = pl.BlockSpec(memory_space=pltpu.SMEM)
ANY = pl.BlockSpec(memory_space=pl.ANY)


def shifted(value, axis, steps):
    count = lax.axis_size(axis)
    return lax.ppermute(value, axis, [(i, (i + steps) % count) for i in range(count)])


def exchange(faces):
    return (
        shifted(faces[1], "cluster", 1),
        shifted(faces[0], "cluster", -1),
        shifted(faces[3], "sub", 1),
        shifted(faces[2], "sub", -1),
        shifted(faces[5], "sub", STRIDE),
        shifted(faces[4], "sub", -STRIDE),
    )


def spread_out(chunks):
    return lax.all_to_all(chunks, AXES, 0, 0, tiled=True)


def call(body, outs, ins, operands, scratch=(), flops=0, moved=0):
    return pl.pallas_call(
        body,
        out_shape=tuple(jax.ShapeDtypeStruct(shape, dtype) for shape, dtype in outs),
        in_specs=list(ins),
        out_specs=tuple(VMEM for _ in outs),
        scratch_shapes=list(scratch),
        compiler_params=pltpu.CompilerParams(vmem_limit_bytes=40 << 20),
        cost_estimate=pl.CostEstimate(flops=flops, bytes_accessed=moved, transcendentals=0),
    )(*operands)


def mapped(part, slots):
    rows = part.shape[0]
    tiles = part.shape[1] // LANES
    pieces = []
    for tile in range(tiles):
        index = jnp.broadcast_to(slots[:, tile * LANES : (tile + 1) * LANES], (rows, LANES))
        inside = index & (LANES - 1)
        out = None
        for source in range(tiles):
            found = jnp.take_along_axis(
                part[:, source * LANES : (source + 1) * LANES],
                inside,
                axis=1,
                mode="promise_in_bounds",
            )
            out = found if out is None else jnp.where(index >= source * LANES, found, out)
        pieces.append(out)
    return jnp.concatenate(pieces, axis=1)


def as_columns(row, width):
    count = row.shape[1]
    tall = jnp.broadcast_to(row, (count, count)).T
    return jnp.concatenate([tall] * (width // count), axis=1)


def row_sums(value):
    total = jnp.sum(value, axis=1, keepdims=True)
    return jnp.broadcast_to(total, (value.shape[0], value.shape[0])).T[0:1]


def column_ids(ids):
    rows = []
    for corner in range(ids.shape[0]):
        for part in range(3):
            rows.append(ids[corner : corner + 1] * 3.0 + float(part))
    return jnp.concatenate(rows, axis=0)


def local(
    load_terms,
    dual_operator,
    dirichlet,
    corner_coupling,
    coarse_inverse,
    face_map,
    face_live,
    corner_ids,
):
    count, size = load_terms.shape[1:]
    face = face_map.shape[2]
    terms = corner_coupling.shape[2]
    corners = corner_ids.shape[1]
    own, coarse = coarse_inverse.shape
    devices = lax.axis_size("cluster") * lax.axis_size("sub")
    tiles = -(-coarse // LANES)
    wide = tiles * LANES
    sent = 8 * (-(-(own + 2) // 8))
    gathered = 8 * (-(-(own * (1 + tiles)) // 8))
    coupling = corner_coupling[0].T
    operator = dual_operator[0]
    precond = dirichlet[0]
    loads = load_terms[0]
    slots = face_map[0]
    field = (count, size)
    part = (count, face)
    longer = count + terms + corners
    matmul_flops = 2 * count * size * size

    def cut(index):
        return slice(index * face, (index + 1) * face)

    def fetch(matrix, held, sems):
        copies = []
        for index in range(6):
            copy = pltpu.make_async_copy(
                matrix.at[pl.ds(index * face, face)],
                held.at[pl.ds(index * face, face)],
                sems.at[index],
            )
            copy.start()
            copies.append(copy)
        return copies

    matrix_scratch = [pltpu.VMEM((size, size), BF16), pltpu.SemaphoreType.DMA((6,))]

    def first_faces(loads_ref, coupling_ref, ids_ref, *outs):
        for index in range(6):
            outs[index][0:count] = loads_ref[:, cut(index)]
            outs[index][count : count + terms] = coupling_ref[:, cut(index)].astype(F32)
            for corner in range(corners):
                outs[index][count + terms + corner : count + terms + corner + 1] = jnp.full(
                    (1, face), ids_ref[0, corner].astype(F32)
                )

    def start(loads_ref, *refs):
        received = refs[0:6]
        slots_ref, live_ref, matrix, residual_ref = refs[6:10]
        faces = refs[10:16]
        dot_ref, held, sems = refs[16:19]
        copies = fetch(matrix, held, sems)
        total = None
        for index in range(6):
            live = live_ref[0, index].astype(F32)
            value = loads_ref[:, cut(index)] + mapped(
                received[index][0:count], slots_ref[index : index + 1]
            )
            value = value * live
            residual_ref[:, cut(index)] = value
            copies[index].wait()
            product = jnp.dot(value.astype(BF16), held[cut(index)], preferred_element_type=F32)
            total = product if total is None else total + product
        for index in range(6):
            faces[index][...] = total[:, cut(index)]
        dot_ref[...] = jnp.broadcast_to(row_sums(total * residual_ref[...]), dot_ref.shape)

    def to_targets(ids_ref, coupling_ref, rounded, rows, chunks_ref):
        corner_rows = lax.dot_general(
            coupling_ref[...], rounded, (((1,), (1,)), ((), ())), preferred_element_type=F32
        )
        extra = jnp.concatenate(rows + [jnp.zeros_like(rows[0])] * (8 - len(rows)), axis=0)
        stacked = jnp.concatenate([corner_rows, extra], axis=0)
        shape = (devices * sent, terms + 8)
        line = lax.broadcasted_iota(jnp.int32, shape, 0)
        lane = lax.broadcasted_iota(jnp.int32, (1, terms + 8), 1)
        target = jnp.full((1, terms + 8), -1, jnp.int32)
        for corner in range(corners):
            for component in range(3):
                number = ids_ref[0, corner] * 3 + component
                place = (number // own) * sent + number % own
                target = jnp.where(lane == corner * 3 + component, place, target)
        chosen = line == target
        within = line % sent
        column = lax.broadcasted_iota(jnp.int32, shape, 1)
        for at in range(len(rows)):
            chosen = chosen | ((column == terms + at) & (within == own + at))
        block = jnp.dot(
            chosen.astype(F32), stacked, precision=EXACT, preferred_element_type=F32
        )
        chunks_ref[...] = block.reshape(devices, sent, count)

    def apply_operator(direction_faces, copies, held):
        total = None
        for index in range(6):
            copies[index].wait()
            product = jnp.dot(direction_faces[index], held[cut(index)], preferred_element_type=F32)
            total = product if total is None else total + product
        return total

    def first_image(*refs):
        own_faces, received = refs[0:6], refs[6:12]
        slots_ref, live_ref, matrix, coupling_ref, ids_ref, dot_ref = refs[12:18]
        direction_ref = refs[18]
        faces = refs[19:25]
        chunks_ref, held, sems = refs[25:28]
        copies = fetch(matrix, held, sems)
        rounded = []
        for index in range(6):
            live = live_ref[0, index].astype(F32)
            value = own_faces[index][...] + mapped(
                received[index][...], slots_ref[index : index + 1]
            )
            value = value * live
            direction_ref[:, cut(index)] = value
            rounded.append(value.astype(BF16))
        total = apply_operator(rounded, copies, held)
        for index in range(6):
            faces[index][...] = total[:, cut(index)]
        curve = row_sums(total * direction_ref[...])
        to_targets(
            ids_ref, coupling_ref, jnp.concatenate(rounded, axis=1), [dot_ref[0:1], curve], chunks_ref
        )

    def next_image(*refs):
        own_faces, received = refs[0:6], refs[6:12]
        slots_ref, live_ref, matrix, coupling_ref, ids_ref = refs[12:17]
        before_ref, dots_ref, totals_ref = refs[17:20]
        direction_ref = refs[20]
        faces = refs[21:27]
        chunks_ref, new_ref, held, sems = refs[27:31]
        copies = fetch(matrix, held, sems)
        new_dot = jnp.sum(dots_ref[...], axis=0)[0:1]
        new_ref[...] = jnp.broadcast_to(new_dot, new_ref.shape)
        ratio = as_columns(new_dot / totals_ref[own : own + 1], face)
        rounded = []
        for index in range(6):
            live = live_ref[0, index].astype(F32)
            value = own_faces[index][...] + mapped(
                received[index][...], slots_ref[index : index + 1]
            )
            value = value * live + ratio * before_ref[:, cut(index)]
            direction_ref[:, cut(index)] = value
            rounded.append(value.astype(BF16))
        total = apply_operator(rounded, copies, held)
        for index in range(6):
            faces[index][...] = total[:, cut(index)]
        curve = row_sums(total * direction_ref[...])
        to_targets(
            ids_ref, coupling_ref, jnp.concatenate(rounded, axis=1), [curve, curve], chunks_ref
        )

    def relay(with_inverse, chunks_ref, *refs):
        totals = jnp.sum(chunks_ref[...], axis=0)
        if with_inverse:
            inverse_ref, out_ref, totals_ref = refs
            rows = [totals[0:own]]
            for tile in range(tiles):
                piece = inverse_ref[:, tile * LANES : min((tile + 1) * LANES, coarse)]
                if piece.shape[1] < LANES:
                    piece = jnp.concatenate(
                        [piece, jnp.zeros((own, LANES - piece.shape[1]), F32)], axis=1
                    )
                rows.append(piece)
            rest = gathered - own * (1 + tiles)
            if rest:
                rows.append(jnp.zeros((rest, LANES), F32))
            out_ref[...] = jnp.broadcast_to(jnp.concatenate(rows, axis=0)[None], out_ref.shape)
        else:
            out_ref, totals_ref = refs
            out_ref[...] = jnp.broadcast_to(totals[None], out_ref.shape)
        totals_ref[...] = totals

    def corner_values(load, inverse, numbers):
        solved = jnp.dot(inverse, load, precision=EXACT, preferred_element_type=F32)
        energy = jnp.sum(solved * load[0:coarse], axis=0, keepdims=True)
        lane = lax.broadcasted_iota(jnp.int32, (terms, coarse), 1).astype(F32)
        values = []
        for number in numbers:
            chosen = (lane == number).astype(F32)
            values.append(
                jnp.dot(chosen, solved, precision=EXACT, preferred_element_type=F32).astype(BF16)
            )
        return values, energy

    def coarse_part(value, coupling_rows):
        return lax.dot_general(
            value, coupling_rows, (((0,), (0,)), ((), ())), preferred_element_type=F32
        )

    def numbers_of(ids, width):
        return column_ids(jnp.broadcast_to(ids[:, 0:1], (corners, width)))

    def gather_load(gathered_ref, load_ref):
        for device in range(devices):
            load_ref[device * own : (device + 1) * own] = gathered_ref[device, 0:own]
        if wide > coarse:
            load_ref[coarse:wide] = jnp.zeros((wide - coarse, count), F32)

    def image_face(index, faces, received, own_first, other_first, slots_ref, live_ref, values):
        live = live_ref[0, index].astype(F32)
        slots_row = slots_ref[index : index + 1]
        other = mapped(other_first[index][count : count + terms], slots_row).astype(BF16)
        value = faces[index][...] + mapped(received[index][...], slots_row)
        value = value + coarse_part(values[0], own_first[:, cut(index)])
        value = value + coarse_part(values[1 + index], other)
        return value * live

    def all_values(load_ref, inverse, ids_ref, other_first):
        corner_rows = [jnp.full((1, coarse), ids_ref[0, c].astype(F32)) for c in range(corners)]
        numbers = [column_ids(jnp.concatenate(corner_rows, axis=0))]
        for index in range(6):
            numbers.append(numbers_of(other_first[index][count + terms : longer], coarse))
        return corner_values(load_ref[...], inverse, numbers)

    def second_residual(*refs):
        faces, received, other_first = refs[0:6], refs[6:12], refs[12:18]
        slots_ref, live_ref, matrix, coupling_ref, ids_ref = refs[18:23]
        before_ref, gathered_ref, totals_ref = refs[23:26]
        residual_ref = refs[26]
        outs = refs[27:33]
        chunks_ref, inverse_ref, step_ref, load_ref, held, sems = refs[33:39]
        copies = fetch(matrix, held, sems)
        gather_load(gathered_ref, load_ref)
        for device in range(devices):
            for tile in range(tiles):
                inverse_ref[
                    device * own : (device + 1) * own, tile * LANES : (tile + 1) * LANES
                ] = gathered_ref[device, own * (1 + tile) : own * (2 + tile)]
        values, energy = all_values(load_ref, inverse_ref[...], ids_ref, other_first)
        step = totals_ref[own : own + 1] / (totals_ref[own + 1 : own + 2] + energy)
        step_ref[...] = jnp.broadcast_to(step, step_ref.shape)
        scale = as_columns(step, face)
        total = None
        for index in range(6):
            image = image_face(
                index, faces, received, coupling_ref, other_first, slots_ref, live_ref, values
            )
            value = before_ref[:, cut(index)] - scale * image
            residual_ref[:, cut(index)] = value
            copies[index].wait()
            product = jnp.dot(value.astype(BF16), held[cut(index)], preferred_element_type=F32)
            total = product if total is None else total + product
        for index in range(6):
            outs[index][...] = total[:, cut(index)]
        chunks_ref[...] = jnp.broadcast_to(
            row_sums(total * residual_ref[...])[None], chunks_ref.shape
        )

    def finish(*refs):
        faces, received, other_first = refs[0:6], refs[6:12], refs[12:18]
        slots_ref, live_ref, coupling_ref, ids_ref = refs[18:22]
        before_ref, gathered_ref, totals_ref, inverse_ref = refs[22:26]
        first_ref, second_ref, step_ref, fresh_ref = refs[26:30]
        multipliers_ref, residual_ref, load_ref = refs[30:33]
        gather_load(gathered_ref, load_ref)
        values, energy = all_values(load_ref, inverse_ref[...], ids_ref, other_first)
        step = fresh_ref[0:1] / (totals_ref[own + 1 : own + 2] + energy)
        scale = as_columns(step, face)
        earlier = as_columns(step_ref[0:1], face)
        for index in range(6):
            image = image_face(
                index, faces, received, coupling_ref, other_first, slots_ref, live_ref, values
            )
            residual_ref[:, cut(index)] = before_ref[:, cut(index)] - scale * image
            multipliers_ref[:, cut(index)] = (
                earlier * first_ref[:, cut(index)] + scale * second_ref[:, cut(index)]
            )

    six = [(part, F32)] * 6
    row = ((8, count), F32)
    sent_block = ((devices, sent, count), F32)
    fixed = [VMEM, SMEM]

    opening = call(
        first_faces, [((longer, face), F32)] * 6, [VMEM, VMEM, SMEM], (loads, coupling, corner_ids)
    )
    other_first = exchange(opening)
    residual, *faces, dot = call(
        start,
        [(field, F32)] + six + [row],
        [VMEM] * 7 + fixed + [ANY],
        (loads, *other_first, slots, face_live, precond),
        matrix_scratch,
        flops=matmul_flops,
    )
    received = exchange(faces)
    direction, *images, chunks = call(
        first_image,
        [(field, F32)] + six + [sent_block],
        [VMEM] * 12 + fixed + [ANY, VMEM, SMEM, VMEM],
        (*faces, *received, slots, face_live, operator, coupling, corner_ids, dot),
        matrix_scratch,
        flops=matmul_flops,
    )
    arrived = exchange(images)
    block, totals = call(
        functools.partial(relay, True),
        [((devices, gathered, count), F32), ((sent, count), F32)],
        [VMEM, VMEM],
        (spread_out(chunks), coarse_inverse),
    )
    second, *faces, dots, inverse, step = call(
        second_residual,
        [(field, F32)] + six + [((devices, 1, count), F32), ((coarse, wide), F32), row],
        [VMEM] * 18 + fixed + [ANY, VMEM, SMEM, VMEM, VMEM, VMEM],
        (
            *images,
            *arrived,
            *other_first,
            slots,
            face_live,
            precond,
            coupling,
            corner_ids,
            residual,
            spread_out(block),
            totals,
        ),
        [pltpu.VMEM((wide, count), F32)] + matrix_scratch,
        flops=matmul_flops,
    )
    received = exchange(faces)
    following, *images, chunks, fresh = call(
        next_image,
        [(field, F32)] + six + [sent_block, row],
        [VMEM] * 12 + fixed + [ANY, VMEM, SMEM, VMEM, VMEM, VMEM],
        (
            *faces,
            *received,
            slots,
            face_live,
            operator,
            coupling,
            corner_ids,
            direction,
            spread_out(dots),
            totals,
        ),
        matrix_scratch,
        flops=matmul_flops,
    )
    arrived = exchange(images)
    block, totals = call(
        functools.partial(relay, False),
        [sent_block, ((sent, count), F32)],
        [VMEM],
        (spread_out(chunks),),
    )
    multipliers, last = call(
        finish,
        [(field, F32)] * 2,
        [VMEM] * 18 + fixed + [VMEM, SMEM] + [VMEM] * 8,
        (
            *images,
            *arrived,
            *other_first,
            slots,
            face_live,
            coupling,
            corner_ids,
            second,
            spread_out(block),
            totals,
            inverse,
            direction,
            following,
            step,
            fresh,
        ),
        [pltpu.VMEM((wide, count), F32)],
    )
    return (multipliers[None], last[None])


def solution(mesh):
    placed = (
        P(AXES, None, None),
        P(AXES, None, None),
        P(AXES, None, None),
        P(AXES, None, None),
        P(AXES, None),
        P(AXES, None, None),
        P(AXES, None),
        P(AXES, None),
    )
    return jax.shard_map(
        local,
        mesh=mesh,
        in_specs=placed,
        out_specs=(P(AXES, None, None), P(AXES, None, None)),
        check_vma=False,
    )
```

```python
import jax
import jax.numpy as jnp
from jax import lax
from jax.experimental import pallas as pl
from jax.experimental.pallas import tpu as pltpu
from jax.sharding import PartitionSpec as P

STRIDE = 4
LANES = 128
AXES = ("cluster", "sub")
EXACT = lax.Precision.HIGHEST
F32 = jnp.float32
BF16 = jnp.bfloat16
HBM = pl.BlockSpec(memory_space=pltpu.HBM)
NT = (((1,), (1,)), ((), ()))
TN = (((0,), (0,)), ((), ()))


def shifted(value, axis, steps):
    count = lax.axis_size(axis)
    return lax.ppermute(value, axis, [(i, (i + steps) % count) for i in range(count)])


def exchange(faces):
    return [
        shifted(faces[1], "cluster", 1),
        shifted(faces[0], "cluster", -1),
        shifted(faces[3], "sub", 1),
        shifted(faces[2], "sub", -1),
        shifted(faces[5], "sub", STRIDE),
        shifted(faces[4], "sub", -STRIDE),
    ]


def spread_out(chunks):
    return lax.all_to_all(chunks, AXES, 0, 0, tiled=True)


class Loaded:
    def __init__(self, source, held, sems, parts):
        rows = source.shape[0] // parts
        self.held = held
        self.copies = []
        for part in range(parts):
            where = pl.ds(part * rows, rows)
            self.copies.append(
                pltpu.make_async_copy(source.at[where], held.at[where], sems.at[part])
            )
            self.copies[part].start()
        self.waited = [False] * parts

    def ref(self, part=0):
        if not self.waited[part]:
            self.copies[part].wait()
            self.waited[part] = True
        return self.held


def run(body, ins, outs, flops=0, parts=None):
    parts = parts or {}
    names = list(ins)
    results = list(outs)
    pieces = [parts.get(name, 1) for name in names]

    def kernel(*refs):
        sources = refs[: len(names)]
        targets = refs[len(names) : len(names) + len(results)]
        rest = refs[len(names) + len(results) :]
        held = rest[: len(names)]
        made = rest[len(names) : len(names) + len(results)]
        sems = rest[len(names) + len(results) : 2 * len(names) + len(results)]
        out_sems = rest[-1]
        loaded = {}
        for at, name in enumerate(names):
            loaded[name] = Loaded(sources[at], held[at], sems[at], pieces[at])
        buffers = dict(zip(results, made, strict=True))
        started = []

        def send(name):
            at = results.index(name)
            copy = pltpu.make_async_copy(made[at], targets[at], out_sems.at[at])
            copy.start()
            started.append(copy)

        body(lambda name, part=0: loaded[name].ref(part), buffers, send)
        for name in names:
            for part in range(parts.get(name, 1)):
                loaded[name].ref(part)
        for copy in started:
            copy.wait()

    moved = sum(v.size * v.dtype.itemsize for v in ins.values())
    out = pl.pallas_call(
        kernel,
        out_shape=tuple(jax.ShapeDtypeStruct(*outs[name]) for name in results),
        in_specs=[HBM] * len(names),
        out_specs=tuple(HBM for _ in results),
        scratch_shapes=[pltpu.VMEM(ins[name].shape, ins[name].dtype) for name in names]
        + [pltpu.VMEM(*outs[name]) for name in results]
        + [pltpu.SemaphoreType.DMA((count,)) for count in pieces]
        + [pltpu.SemaphoreType.DMA((len(results),))],
        compiler_params=pltpu.CompilerParams(vmem_limit_bytes=67043328),
        cost_estimate=pl.CostEstimate(flops=flops, bytes_accessed=moved, transcendentals=0),
    )(*ins.values())
    return dict(zip(results, out, strict=True))


def mapped(part, slots):
    rows = part.shape[0]
    tiles = part.shape[1] // LANES
    pieces = []
    for tile in range(tiles):
        index = jnp.broadcast_to(slots[:, tile * LANES : (tile + 1) * LANES], (rows, LANES))
        inside = index & (LANES - 1)
        out = None
        for source in range(tiles):
            found = jnp.take_along_axis(
                part[:, source * LANES : (source + 1) * LANES],
                inside,
                axis=1,
                mode="promise_in_bounds",
            )
            out = found if out is None else jnp.where(index >= source * LANES, found, out)
        pieces.append(out)
    return jnp.concatenate(pieces, axis=1)


def as_columns(row, width):
    count = row.shape[1]
    tall = jnp.broadcast_to(row, (count, count)).T
    return jnp.concatenate([tall] * (width // count), axis=1)


def row_sums(value):
    total = jnp.sum(value, axis=1, keepdims=True)
    return jnp.broadcast_to(total, (value.shape[0], value.shape[0])).T[0:1]


def local(
    load_terms,
    dual_operator,
    dirichlet,
    corner_coupling,
    coarse_inverse,
    face_map,
    face_live,
    corner_ids,
):
    count, size = load_terms.shape[1:]
    face = face_map.shape[2]
    terms = corner_coupling.shape[2]
    corners = corner_ids.shape[1]
    own, coarse = coarse_inverse.shape
    devices = lax.axis_size("cluster") * lax.axis_size("sub")
    assert own == 3
    tiles = -(-coarse // LANES)
    wide = tiles * LANES
    sent = 8
    at_curve = own * (1 + tiles)
    gathered = 8 * (-(-(at_curve + 2) // 8))
    named = 7 * terms
    coupling = corner_coupling[0].T
    field = ((count, size), F32)
    part = ((count, face), F32)
    longer = count + terms + corners
    matmul_flops = 2 * count * size * size
    six = {"face%d" % index: part for index in range(6)}
    rows8 = ((8, count), F32)
    sent_block = ((devices, sent, count), F32)

    def cut(index):
        return slice(index * face, (index + 1) * face)

    def opening(loads_ref, coupling_ref, live_ref, ids_ref, *outs):
        for index in range(6):
            outs[index][0:count] = loads_ref[:, cut(index)]
            outs[index][count : count + terms] = coupling_ref[:, cut(index)].astype(F32)
            for corner in range(corners):
                outs[index][count + terms + corner : count + terms + corner + 1] = jnp.full(
                    (1, face), ids_ref[0, corner].astype(F32)
                )
        info = outs[6]
        for index in range(6):
            info[index : index + 1] = jnp.full((1, face), live_ref[0, index].astype(F32))
        info[6:8] = jnp.zeros((2, face), F32)
        for corner in range(corners):
            info[8 + corner : 9 + corner] = jnp.full((1, face), ids_ref[0, corner].astype(F32))

    def numbers_of(ids):
        made = []
        for corner in range(corners):
            for component in range(3):
                made.append(ids[corner : corner + 1] * 3.0 + float(component))
        return jnp.concatenate(made, axis=0)

    def assembled(get, index, own_part, received):
        slots = get("slots")[index : index + 1]
        return (own_part + mapped(received, slots)) * get("info")[index : index + 1]

    def times_matrix(get, total, index, value):
        product = jnp.dot(
            value.astype(BF16), get("matrix", index)[cut(index)], preferred_element_type=F32
        )
        return product if total is None else total + product

    def scatter_loads(get, image, couplings, numbers, dot):
        first = None
        others = []
        for index in range(6):
            value = image[:, cut(index)] * get("info")[index : index + 1]
            high = value.astype(BF16)
            low = (value - high.astype(F32)).astype(BF16)
            both = lax.dot_general(
                couplings(index),
                jnp.concatenate([high, low], axis=0),
                NT,
                preferred_element_type=F32,
            )
            both = both[:, 0:count] + both[:, count : 2 * count]
            first = both[0:terms] if first is None else first + both[0:terms]
            others.append(both[terms : 2 * terms])
        stacked = jnp.concatenate(
            [first] + others + [dot, jnp.zeros((7, count), F32)], axis=0
        )
        vertex = jnp.floor((numbers + 0.5) * (1.0 / 3.0))
        place = (numbers + vertex * float(sent - 3)).astype(jnp.int32)
        shape = (named + 8, devices * sent)
        place = jnp.concatenate([place] * (shape[1] // LANES), axis=1)
        lane = lax.broadcasted_iota(jnp.int32, shape, 1)
        line = lax.broadcasted_iota(jnp.int32, shape, 0)
        chosen = (line < named) & (lane == place)
        chosen = chosen | ((line == named) & ((lane & (sent - 1)) == own))
        block = lax.dot_general(
            chosen.astype(F32), stacked, TN, precision=EXACT, preferred_element_type=F32
        )
        return block.reshape(devices, sent, count)

    def gather_chunk(get, totals, extra):
        made = [totals[0:own]]
        for tile in range(tiles):
            piece = get("inverse")[:, tile * LANES : min((tile + 1) * LANES, coarse)]
            if piece.shape[1] < LANES:
                piece = jnp.concatenate(
                    [piece, jnp.zeros((own, LANES - piece.shape[1]), F32)], axis=1
                )
            made.append(piece)
        made.extend(extra)
        rest = gathered - at_curve - len(extra)
        if rest:
            made.append(jnp.zeros((rest, LANES), F32))
        return jnp.broadcast_to(
            jnp.concatenate(made, axis=0)[None], (devices, gathered, count)
        )

    def solve_coarse(get):
        block = get("block")
        load = [block[device, 0:own] for device in range(devices)]
        if wide > coarse:
            load.append(jnp.zeros((wide - coarse, count), F32))
        load = jnp.concatenate(load, axis=0)
        solved = None
        for tile in range(tiles):
            begin = own * (1 + tile)
            inverse = jnp.concatenate(
                [block[device, begin : begin + own] for device in range(devices)], axis=0
            )
            product = jnp.dot(
                inverse,
                load[tile * LANES : (tile + 1) * LANES],
                precision=EXACT,
                preferred_element_type=F32,
            )
            solved = product if solved is None else solved + product
        energy = jnp.sum(solved * load[0:coarse], axis=0, keepdims=True)
        lane = lax.broadcasted_iota(jnp.int32, (named, wide), 1)
        numbers = jnp.concatenate([get("numbers")[0:named]] * tiles, axis=1)
        chosen = (lane == numbers.astype(jnp.int32)).astype(F32)
        if wide > coarse:
            solved = jnp.concatenate([solved, jnp.zeros((wide - coarse, count), F32)], axis=0)
        values = jnp.dot(chosen, solved, precision=EXACT, preferred_element_type=F32)
        sums = jnp.sum(block[:, at_curve : at_curve + 2], axis=0)
        return values.astype(BF16), energy, sums

    def image_face(get, index, values):
        begin = terms * (1 + index)
        corner = jnp.concatenate([values[0:terms], values[begin : begin + terms]], axis=0)
        rows = jnp.concatenate(
            [get("coupling")[:, cut(index)], get("other")[:, cut(index)]], axis=0
        )
        back = lax.dot_general(corner, rows, TN, preferred_element_type=F32)
        return assembled(
            get, index, get("face%d" % index)[...] + back, get("received%d" % index)[...]
        )

    def start(get, out, send):
        total = None
        ids = [jnp.broadcast_to(get("info")[8:16][:, 0:1], (corners, LANES))]
        for index in range(6):
            received = get("received%d" % index)
            value = assembled(get, index, get("loads")[:, cut(index)], received[0:count])
            out["residual"][:, cut(index)] = value
            total = times_matrix(get, total, index, value)
        send("residual")
        for index in range(6):
            out["face%d" % index][...] = total[:, cut(index)]
            send("face%d" % index)
        for index in range(6):
            received = get("received%d" % index)
            rows = mapped(received[count : count + terms], get("slots")[index : index + 1])
            out["other"][:, cut(index)] = rows.astype(BF16)
            ids.append(
                jnp.broadcast_to(received[count + terms : longer][:, 0:1], (corners, LANES))
            )
        send("other")
        numbers = jnp.concatenate(
            [numbers_of(value) for value in ids] + [jnp.full((8, LANES), -1.0, F32)], axis=0
        )
        out["numbers"][...] = numbers
        send("numbers")
        out["chunks"][...] = scatter_loads(
            get,
            total,
            lambda index: jnp.concatenate(
                [get("coupling")[:, cut(index)], out["other"][:, cut(index)]], axis=0
            ),
            numbers,
            row_sums(total * out["residual"][...]),
        )
        send("chunks")

    def image(get, out, send, later):
        total = None
        for index in range(6):
            value = assembled(
                get, index, get("face%d" % index)[...], get("received%d" % index)[...]
            )
            out["direction"][:, cut(index)] = value
            total = times_matrix(get, total, index, value)
        send("direction")
        for index in range(6):
            out["face%d" % index][...] = total[:, cut(index)]
            send("face%d" % index)
        extra = [row_sums(total * out["direction"][...])]
        if later:
            extra.append(0.5 * row_sums(out["direction"][...] * get("before")[...]))
        totals = jnp.sum(get("arrived")[...], axis=0)
        out["totals"][...] = totals
        send("totals")
        out["block"][...] = gather_chunk(get, totals, extra)
        send("block")

    def second_residual(get, out, send):
        values, energy, sums = solve_coarse(get)
        dot = get("totals")[own : own + 1]
        curve = sums[0:1] + energy
        step = dot / curve
        out["rows"][...] = jnp.concatenate([step, curve, dot, jnp.zeros((5, count), F32)], axis=0)
        send("rows")
        scale = as_columns(step, face)
        total = None
        for index in range(6):
            product = image_face(get, index, values)
            out["image"][:, cut(index)] = product
            value = get("residual")[:, cut(index)] - scale * product
            out["second"][:, cut(index)] = value
            total = times_matrix(get, total, index, value)
        send("image")
        send("second")
        for index in range(6):
            out["face%d" % index][...] = total[:, cut(index)]
            send("face%d" % index)
        out["chunks"][...] = scatter_loads(
            get,
            total,
            lambda index: jnp.concatenate(
                [get("coupling")[:, cut(index)], get("other")[:, cut(index)]], axis=0
            ),
            get("numbers")[...],
            row_sums(total * out["second"][...]),
        )
        send("chunks")

    def finish(get, out, send):
        values, energy, sums = solve_coarse(get)
        rows = get("rows")
        first, curve, dot = rows[0:1], rows[1:2], rows[2:3]
        new_dot = get("totals")[own : own + 1]
        ratio = new_dot / dot
        step = new_dot / (sums[0:1] + energy + 2.0 * ratio * sums[1:2] + ratio * ratio * curve)
        scale = as_columns(step, face)
        ratio_columns = as_columns(ratio, face)
        earlier = as_columns(first + step * ratio, face)
        for index in range(6):
            out["multipliers"][:, cut(index)] = (
                earlier * get("first")[:, cut(index)] + scale * get("next")[:, cut(index)]
            )
        send("multipliers")
        for index in range(6):
            product = image_face(get, index, values) + ratio_columns * get("before")[:, cut(index)]
            out["last"][:, cut(index)] = get("second")[:, cut(index)] - scale * product
        send("last")

    def received_faces(arrays):
        return {"received%d" % index: value for index, value in enumerate(arrays)}

    def faces_of(result):
        return {"face%d" % index: result["face%d" % index] for index in range(6)}

    def sent_faces(result):
        return received_faces(exchange([result["face%d" % index] for index in range(6)]))

    whole = pl.BlockSpec(memory_space=pltpu.VMEM)
    scalar = pl.BlockSpec(memory_space=pltpu.SMEM)
    *opened, info = pl.pallas_call(
        opening,
        out_shape=tuple([jax.ShapeDtypeStruct((longer, face), F32)] * 6)
        + (jax.ShapeDtypeStruct((8 + corners, face), F32),),
        in_specs=[whole, whole, scalar, scalar],
        out_specs=(whole,) * 7,
        compiler_params=pltpu.CompilerParams(vmem_limit_bytes=67043328),
    )(load_terms[0], coupling, face_live, corner_ids)
    slots = face_map[0]
    fixed = dict(slots=slots, info=info)
    blocks = {"matrix": 6}
    one = run(
        start,
        dict(
            loads=load_terms[0],
            **fixed,
            **received_faces(exchange(opened)),
            coupling=coupling,
            matrix=dirichlet[0],
        ),
        dict(
            residual=field,
            **six,
            other=((terms, size), BF16),
            numbers=((named + 8, LANES), F32),
            chunks=sent_block,
        ),
        matmul_flops,
        blocks,
    )
    received = sent_faces(one)
    arrived = spread_out(one["chunks"])
    gathered_block = ((devices, gathered, count), F32)
    two = run(
        lambda get, out, send: image(get, out, send, False),
        dict(
            **fixed,
            **faces_of(one),
            **received,
            matrix=dual_operator[0],
            arrived=arrived,
            inverse=coarse_inverse,
        ),
        dict(direction=field, **six, totals=rows8, block=gathered_block),
        matmul_flops,
        blocks,
    )
    known = dict(coupling=coupling, other=one["other"], numbers=one["numbers"])
    received = sent_faces(two)
    block = spread_out(two["block"])
    three = run(
        second_residual,
        dict(
            block=block,
            totals=two["totals"],
            **fixed,
            **known,
            **faces_of(two),
            **received,
            residual=one["residual"],
            matrix=dirichlet[0],
        ),
        dict(rows=rows8, image=field, second=field, **six, chunks=sent_block),
        matmul_flops,
        blocks,
    )
    received = sent_faces(three)
    arrived = spread_out(three["chunks"])
    four = run(
        lambda get, out, send: image(get, out, send, True),
        dict(
            **fixed,
            **faces_of(three),
            **received,
            matrix=dual_operator[0],
            before=three["image"],
            arrived=arrived,
            inverse=coarse_inverse,
        ),
        dict(direction=field, **six, totals=rows8, block=gathered_block),
        matmul_flops,
        blocks,
    )
    received = sent_faces(four)
    block = spread_out(four["block"])
    five = run(
        finish,
        dict(
            block=block,
            totals=four["totals"],
            rows=three["rows"],
            **fixed,
            **known,
            first=two["direction"],
            next=four["direction"],
            **faces_of(four),
            **received,
            before=three["image"],
            second=three["second"],
        ),
        dict(multipliers=field, last=field),
    )
    return (five["multipliers"][None], five["last"][None])


def solution(mesh):
    placed = (
        P(AXES, None, None),
        P(AXES, None, None),
        P(AXES, None, None),
        P(AXES, None, None),
        P(AXES, None),
        P(AXES, None, None),
        P(AXES, None),
        P(AXES, None),
    )
    return jax.shard_map(
        local,
        mesh=mesh,
        in_specs=placed,
        out_specs=(P(AXES, None, None), P(AXES, None, None)),
        check_vma=False,
    )
```
